128 devices in a mesh: row: 8 (over y_hi, x), col: 16 (over y_lo, z, core).
Axes of the slice: x: 4, y: 4 (y_hi: 2, y_lo: 2; y = y_hi * 2 + y_lo), z: 4, core: 2. Of those that a mesh axis runs over, the one named last changes fastest.
Arguments:
- adj_tiles: bfloat16 [8, 16, 80, 256, 256], P('row', 'col'), may hold values from -0.0625 to 0.0625
- tile_rows: int32 [8, 16, 80], P('row', 'col'), may hold values from 0 to 15, as said below
- tile_cols: int32 [8, 16, 80], P('row', 'col'), may hold values from 0 to 7
- tile_counts: int32 [8, 16], P('row', 'col'), may hold values from 20 to 80, as said below
- features: bfloat16 [32768, 512], P(('col', 'row')), may hold values from -6 to 6
- weight: bfloat16 [512, 512], replicated, may hold values from -0.25 to 0.25
- node_grad: bfloat16 [32768, 512], P(('row', 'col')), may hold values from -6 to 6
Outputs:
- node_out: bfloat16 [32768, 512], P(('row', 'col'))
- weight_grad: float32 [512, 512], replicated
- feature_grad: bfloat16 [32768, 512], P(('col', 'row'))
The draws below stay inside these ranges and needn't reach their ends.
Inputs may be any that keep to these rules, and one draw needn't show every extreme that they name: Within one cell the first 80 slots name distinct tiles (pairs of tile_rows and tile_cols). `tile_counts`: slots from this number on hold no tile; some cell fills all its slots.
All inputs are finite; a program needn't handle non-finite values.
Results may differ from the reference program's by a relative error of at most 0.027.
Values may be sent and summed in bfloat16 or wider, within the bound.
No kernel may reach another device: no remote copies, remote signals or barrier semaphores. Data moves between devices by JAX's collectives and lax.ppermute only.
A program may use at most 128 MiB of HBM per device.

```python
import jax
import jax.numpy as jnp
from jax import lax

F = 512
H = 512
TILE = 256
GRID_R = 8
GRID_C = 16
NODES = 32768
TROW = 16
TCOL = 8
TMAX = 80
TMIN = 20
N_COL = 16


def cell_positions(key):
    base = jax.random.fold_in(key, 11)
    cell_keys = jax.random.split(base, GRID_R * GRID_C)

    def pick_cell(cell_key):
        return jax.random.permutation(cell_key, TROW * TCOL)[:TMAX]
    picks = jax.vmap(pick_cell)(cell_keys)
    return picks.reshape(GRID_R, GRID_C, TMAX).astype(jnp.int32)


def draw_tile_rows(key, part):
    return cell_positions(key) // TCOL


def draw_tile_cols(key, part):
    return cell_positions(key) % TCOL


def draw_tile_counts(key, part):
    first_key, second_key = jax.random.split(jax.random.fold_in(key, 23))
    level = jax.random.randint(first_key, (GRID_R * GRID_C,), 0, 8)
    counts = TMIN + level * level * (TMAX - TMIN) // 49
    heavy = jax.random.randint(second_key, (), 0, GRID_R * GRID_C)
    places = jnp.arange(GRID_R * GRID_C)
    counts = jnp.where(places == heavy, TMAX, counts)
    return counts.reshape(GRID_R, GRID_C).astype(jnp.int32)


def levels(key, extent, cuts, least, largest):
    gain = 1.0
    for position, blocks in cuts:
        steps = jax.random.uniform(jax.random.fold_in(jax.random.fold_in(key, 6), position), (blocks,), jnp.float32, least / len(cuts), largest / len(cuts))
        gain = gain * jnp.repeat(jnp.exp(steps), extent[position] // blocks).reshape((-1,) + (1,) * (len(extent) - 1 - position))
    return gain


def scatter_about(rng, extent, deviation, most, cuts=(), kind=jnp.bfloat16):
    gain = levels(rng, extent, cuts, -0.22, 0.18) if cuts else 1.0
    drawn = jax.random.normal(rng, extent, jnp.float32) * deviation * gain
    return jnp.minimum(jnp.maximum(drawn, -most), most).astype(kind)


def setup_inputs(seed: int = 0) -> dict:
    splits = jax.random.split(jax.random.key(seed), 8)
    return {
        "adj_tiles": scatter_about(splits[0], (GRID_R, GRID_C, TMAX, TILE, TILE), (TILE * N_COL * TMAX // (2 * TROW)) ** -0.5, 0.0625, ((0, 8), (1, 16))),
        "tile_rows": draw_tile_rows(jax.random.fold_in(splits[7], 71), 0),
        "tile_cols": draw_tile_cols(jax.random.fold_in(splits[7], 71), 0),
        "tile_counts": draw_tile_counts(jax.random.fold_in(splits[7], 71), 0),
        "features": scatter_about(splits[4], (NODES, F), 1.0, 6.0, ((0, 128),)),
        "weight": scatter_about(splits[5], (F, H), F ** -0.5, 0.25),
        "node_grad": scatter_about(splits[6], (NODES, H), 1.0, 6.0, ((0, 128),)),
    }


def cell_forward(cell_tiles, cell_rows, cell_cols, cell_count, source):
    total = jnp.zeros((TROW, TILE, F), jnp.float32)

    def add_tile(slot, running):
        tile = lax.dynamic_index_in_dim(cell_tiles, slot, 0, False)
        block = lax.dynamic_index_in_dim(source, cell_cols[slot], 0, False)
        product = jnp.dot(tile, block, preferred_element_type=jnp.float32)
        return running.at[cell_rows[slot]].add(product)
    return lax.fori_loop(jnp.int32(0), cell_count.astype(jnp.int32), add_tile, total)

def cell_backward(cell_tiles, cell_rows, cell_cols, cell_count, source):
    total = jnp.zeros((TCOL, TILE, F), jnp.float32)

    def add_tile(slot, running):
        tile = lax.dynamic_index_in_dim(cell_tiles, slot, 0, False)
        block = lax.dynamic_index_in_dim(source, cell_rows[slot], 0, False)
        product = jnp.dot(tile.T, block, preferred_element_type=jnp.float32)
        return running.at[cell_cols[slot]].add(product)
    return lax.fori_loop(jnp.int32(0), cell_count.astype(jnp.int32), add_tile, total)

def rounded(values):
    return lax.optimization_barrier(values.astype(jnp.bfloat16)).astype(jnp.float32)

def reference(adj_tiles, tile_rows, tile_cols, tile_counts, features, weight, node_grad):
    column_feats = features.reshape(GRID_C, TCOL, TILE, F)

    def row_block(row_index):

        def add_cell(col_index, running):
            part = cell_forward(adj_tiles[row_index, col_index], tile_rows[row_index, col_index], tile_cols[row_index, col_index], tile_counts[row_index, col_index], column_feats[col_index])
            return running + rounded(part)
        return lax.fori_loop(0, GRID_C, add_cell, jnp.zeros((TROW, TILE, F), jnp.float32))
    agg = lax.map(row_block, jnp.arange(GRID_R, dtype=jnp.int32)).reshape(NODES, F)
    agg_b = agg.astype(jnp.bfloat16)
    pre = jnp.dot(agg_b, weight, preferred_element_type=jnp.float32)
    node_out = jax.nn.silu(pre).astype(jnp.bfloat16)
    sigma = jax.nn.sigmoid(pre)
    dpre = (node_grad.astype(jnp.float32) * sigma * (1.0 + pre * (1.0 - sigma))).astype(jnp.bfloat16)
    weight_grad = jnp.dot(agg_b.T, dpre, preferred_element_type=jnp.float32) / jnp.sqrt(jnp.float32(NODES))
    dagg = jnp.dot(dpre, weight.T, preferred_element_type=jnp.float32).astype(jnp.bfloat16)
    grad_blocks = dagg.reshape(GRID_R, TROW, TILE, F)

    def col_block(col_index):

        def add_cell(row_index, running):
            part = cell_backward(adj_tiles[row_index, col_index], tile_rows[row_index, col_index], tile_cols[row_index, col_index], tile_counts[row_index, col_index], grad_blocks[row_index])
            return running + rounded(part)
        return lax.fori_loop(0, GRID_R, add_cell, jnp.zeros((TCOL, TILE, F), jnp.float32))
    feature_grad = lax.map(col_block, jnp.arange(GRID_C, dtype=jnp.int32)).reshape(NODES, F).astype(jnp.bfloat16)
    return (node_out, weight_grad, feature_grad)
```

```python
import jax
import jax.numpy as jnp
from jax import lax
from jax.experimental import pallas as pl
from jax.experimental.pallas import tpu as pltpu
from jax.sharding import PartitionSpec as P

BF = jnp.bfloat16
F32 = jnp.float32
GROUP = 4
SMEM = pl.BlockSpec(memory_space=pltpu.SMEM)
ANY = pl.BlockSpec(memory_space=pl.ANY)


def list_tiles(dest, source, count, total, dests, first, slots, srcs, fill):
    for d in range(dests):
        fill[d] = 0

    def tally(t, carry):
        fill[dest[t]] = fill[dest[t]] + 1
        return carry

    lax.fori_loop(0, count, tally, 0)

    def place(d, pos):
        first[d] = pos
        groups = jnp.maximum(lax.div(fill[d] + (GROUP - 1), GROUP), 1)
        fill[d] = pos * GROUP
        for k in range(GROUP):
            last = (pos + groups - 1) * GROUP + k
            slots[last] = total
            srcs[last] = 0
        return pos + groups

    first[dests] = lax.fori_loop(0, dests, place, 0)

    def put(t, carry):
        d = dest[t]
        p = fill[d]
        fill[d] = p + 1
        slots[p] = t
        srcs[p] = source[t]
        return carry

    lax.fori_loop(0, count, put, 0)


def schedule(rows, cols, count, row_tiles, col_tiles):
    total = rows.shape[0]

    def body(r, c, n, ff, fs, fc, bf, bs, bc, fill):
        list_tiles(r, c, n[0], total, row_tiles, ff, fs, fc, fill)
        list_tiles(c, r, n[0], total, col_tiles, bf, bs, bc, fill)

    def table(n):
        return jax.ShapeDtypeStruct((n,), jnp.int32)

    fl = total + row_tiles * GROUP
    bl = total + col_tiles * GROUP
    return pl.pallas_call(
        body,
        in_specs=[SMEM] * 3,
        out_specs=[SMEM] * 6,
        out_shape=[table(row_tiles + 1), table(fl), table(fl)]
        + [table(col_tiles + 1), table(bl), table(bl)],
        scratch_shapes=[pltpu.SMEM((max(row_tiles, col_tiles),), jnp.int32)],
        name="schedule",
    )(rows, cols, count)


def spread(first, slots, srcs, tiles, sources, start, dests, transposed):
    total, size = tiles.shape[:2]
    room = slots.shape[0]
    blocks = sum(s.shape[0] for s in sources)
    block = sources[0].shape[1:]

    def body(*refs):
        first, slots, srcs, tiles = refs[:4]
        ins = refs[4 : 4 + len(sources)]
        out, held, src, acc, stage, tile_sem, src_sem, out_sem = refs[4 + len(sources) :]
        base = first[start] * GROUP
        end = first[start + dests] * GROUP
        copies = []
        at = 0
        for k, ref in enumerate(ins):
            n = ref.shape[0]
            copies.append(pltpu.make_async_copy(ref, src.at[pl.ds(at, n)], src_sem.at[k]))
            at += n
        for copy in copies:
            copy.start()

        def fetch(p, carry):
            s = slots[base + p]

            @pl.when(s < total)
            def _():
                pltpu.make_async_copy(tiles.at[s], held.at[p], tile_sem.at[p]).start()

            @pl.when(s >= total)
            def _():
                held[p] = jnp.zeros((size, size), BF)

            return carry

        lax.fori_loop(0, end - base, fetch, 0)
        for copy in copies:
            copy.wait()

        def product(g):
            ps = [g * GROUP + k for k in range(GROUP)]
            for p in ps:

                @pl.when(slots[p] < total)
                def _():
                    pltpu.make_async_copy(
                        tiles.at[0], held.at[p - base], tile_sem.at[p - base]
                    ).wait()

            if transposed:
                left = jnp.concatenate([src[srcs[p]] for p in ps], 1)
                right = held[pl.ds(g * GROUP - base, GROUP)].reshape(GROUP * size, size)
            else:
                left = jnp.concatenate([held[p - base] for p in ps], 1)
                right = jnp.concatenate([src[srcs[p]] for p in ps], 0)
            return jnp.dot(left, right, preferred_element_type=F32)

        def one(d, carry):
            lo = first[start + d]
            acc[...] = product(lo)

            def more(g, inner):
                acc[...] += product(g)
                return inner

            lax.fori_loop(lo + 1, first[start + d + 1], more, 0)
            stage[d] = acc[...].astype(BF)
            pltpu.make_async_copy(stage.at[d], out.at[d], out_sem.at[d]).start()
            return carry

        lax.fori_loop(0, dests, one, 0)

        def finish(d, carry):
            pltpu.make_async_copy(stage.at[d], out.at[d], out_sem.at[d]).wait()
            return carry

        lax.fori_loop(0, dests, finish, 0)

    return pl.pallas_call(
        body,
        in_specs=[SMEM] * 3 + [ANY] * (1 + len(sources)),
        out_specs=ANY,
        out_shape=jax.ShapeDtypeStruct((dests,) + block, BF),
        scratch_shapes=[
            pltpu.VMEM((room, size, size), BF),
            pltpu.VMEM((blocks,) + block, BF),
            pltpu.VMEM(block, F32),
            pltpu.VMEM((dests,) + block, BF),
            pltpu.SemaphoreType.DMA((room,)),
            pltpu.SemaphoreType.DMA((len(sources),)),
            pltpu.SemaphoreType.DMA((dests,)),
        ],
        compiler_params=pltpu.CompilerParams(vmem_limit_bytes=56 * 1024 * 1024),
        name="spread_back" if transposed else "spread",
    )(first, slots, srcs, tiles, *sources)


def local(adj_tiles, tile_rows, tile_cols, tile_counts, features, weight, node_grad):
    tiles = adj_tiles[0, 0]
    size = tiles.shape[1]
    width = features.shape[1]
    row_devices = lax.axis_size("row")
    col_devices = lax.axis_size("col")
    half = col_devices // 2
    core = lax.rem(lax.axis_index("col"), 2)
    same_core = [[2 * k + c for k in range(half)] for c in range(2)]
    swap = [(i, i ^ 1) for i in range(col_devices)]
    rows = tile_rows[0, 0]
    rows = lax.shift_right_logical(rows, 1) + half * ((rows & 1) ^ core)
    ff, fs, fc, bf, bs, bc = schedule(
        rows, tile_cols[0, 0], tile_counts[0], col_devices, row_devices
    )

    spread_feats = jnp.broadcast_to(features[None], (row_devices, size, width))
    column_feats = lax.all_to_all(spread_feats, "row", 0, 0)
    sent = spread(ff, fs, fc, tiles, [column_feats], half, half, False)
    met = lax.ppermute(sent, "col", swap)
    kept = spread(ff, fs, fc, tiles, [column_feats], 0, half, False)
    pair = (kept.astype(F32) + met.astype(F32)).astype(BF)
    parts = lax.all_to_all(pair, "col", 0, 0, axis_index_groups=same_core)
    agg = parts.astype(F32).sum(0).astype(BF)

    pre = jnp.dot(agg, weight, preferred_element_type=F32)
    node_out = jax.nn.silu(pre).astype(BF)
    sigma = jax.nn.sigmoid(pre)
    dpre = (node_grad.astype(F32) * sigma * (1.0 + pre * (1.0 - sigma))).astype(BF)
    dagg = lax.dot_general(
        weight, dpre, (((1,), (1,)), ((), ())), preferred_element_type=F32
    ).astype(BF)
    scale = 1.0 / jnp.sqrt(jnp.float32(size * row_devices * col_devices))
    term = lax.dot_general(agg, dpre, (((0,), (0,)), ((), ())), preferred_element_type=F32)

    own = lax.all_to_all(
        jnp.broadcast_to(dagg[None], (half,) + dagg.shape),
        "col",
        0,
        0,
        axis_index_groups=same_core,
    )
    other = lax.ppermute(own, "col", swap)
    back = spread(bf, bs, bc, tiles, [own, other], 0, row_devices, True)
    back = lax.all_to_all(back, "row", 0, 0)
    feature_grad = back.astype(F32).sum(0).T.astype(BF)

    term = (term * scale).reshape((2,) + (term.shape[0] // 2, term.shape[1]))
    mine = lax.dynamic_index_in_dim(term, core, 0, False)
    yours = lax.dynamic_index_in_dim(term, 1 - core, 0, False)
    mine = mine + lax.ppermute(yours, "col", swap)
    mine = mine.reshape(half, mine.shape[0] // half, mine.shape[1])
    mine = lax.all_to_all(mine, "col", 0, 0, axis_index_groups=same_core).sum(0)
    mine = lax.all_to_all(
        jnp.broadcast_to(mine[None], (row_devices,) + mine.shape), "row", 0, 0
    ).sum(0)
    mine = lax.all_to_all(
        jnp.broadcast_to(mine[None], (half,) + mine.shape),
        "col",
        0,
        0,
        axis_index_groups=same_core,
    ).reshape(weight.shape[0] // 2, weight.shape[1])
    yours = lax.ppermute(mine, "col", swap)
    weight_grad = jnp.where(
        core == 0, jnp.concatenate([mine, yours], 0), jnp.concatenate([yours, mine], 0)
    )
    return node_out, weight_grad, feature_grad


def solution(mesh):
    in_specs = (
        P("row", "col", None, None, None),
        P("row", "col", None),
        P("row", "col", None),
        P("row", "col"),
        P(("col", "row"), None),
        P(),
        P(("row", "col"), None),
    )
    out_specs = (P(("row", "col"), None), P(), P(("col", "row"), None))
    return jax.shard_map(local, mesh=mesh, in_specs=in_specs, out_specs=out_specs, check_vma=False)
```

```python
import jax
import jax.numpy as jnp
from jax import lax
from jax.experimental import pallas as pl
from jax.experimental.pallas import tpu as pltpu
from jax.sharding import PartitionSpec as P

BF = jnp.bfloat16
F32 = jnp.float32
GROUP = 2
RING = 4
CHUNKS = 8
SMEM = pl.BlockSpec(memory_space=pltpu.SMEM)
VMEM = pl.BlockSpec(memory_space=pltpu.VMEM)
HBM = pl.BlockSpec(memory_space=pltpu.HBM)


def room(total, dests):
    return total + dests * GROUP


def list_tiles(dest, source, count, total, dests, blank, table, fill):
    slots = dests + 1
    srcs = slots + room(total, dests)
    for d in range(dests):
        fill[d] = 0

    def tally(t, carry):
        fill[dest[t]] = fill[dest[t]] + 1
        return carry

    lax.fori_loop(0, count, tally, 0)

    def place(d, pos):
        table[d] = pos
        groups = jnp.maximum(lax.div(fill[d] + (GROUP - 1), GROUP), 1)
        fill[d] = pos * GROUP
        for k in range(GROUP):
            last = (pos + groups - 1) * GROUP + k
            table[slots + last] = 0
            table[srcs + last] = blank
        return pos + groups

    table[dests] = lax.fori_loop(0, dests, place, 0)

    def put(t, carry):
        d = dest[t]
        p = fill[d]
        fill[d] = p + 1
        table[slots + p] = t
        table[srcs + p] = source[t]
        return carry

    lax.fori_loop(0, count, put, 0)


def tile_copies(tiles, held, count, sem):
    total = tiles.shape[0]
    chunk = -(-total // CHUNKS)
    cuts = [(at, min(chunk, total - at)) for at in range(0, total, chunk)]
    copies = [
        pltpu.make_async_copy(tiles.at[pl.ds(at, n)], held.at[pl.ds(at, n)], sem.at[k])
        for k, (at, n) in enumerate(cuts)
    ]
    for (at, _), copy in zip(cuts, copies):
        pl.when(at < count)(copy.start)

    def wait():
        for (at, _), copy in zip(cuts, copies):
            pl.when(at < count)(copy.wait)

    return wait


def schedule(fdest, fsource, bdest, bsource, count, tiles, row_tiles, col_tiles):
    total = fdest.shape[0]

    def body(fd, fr, bd, br, n, tiles, forward, backward, held, fill, sem):
        wait = tile_copies(tiles, held, n[0], sem)
        list_tiles(fd, fr, n[0], total, row_tiles, col_tiles, forward, fill)
        list_tiles(bd, br, n[0], total, col_tiles, row_tiles, backward, fill)
        wait()

    def table(dests):
        return jax.ShapeDtypeStruct((dests + 1 + 2 * room(total, dests),), jnp.int32)

    return pl.pallas_call(
        body,
        in_specs=[SMEM] * 5 + [HBM],
        out_specs=[SMEM] * 2 + [VMEM],
        out_shape=[
            table(row_tiles),
            table(col_tiles),
            jax.ShapeDtypeStruct(tiles.shape, tiles.dtype),
        ],
        scratch_shapes=[
            pltpu.SMEM((max(row_tiles, col_tiles),), jnp.int32),
            pltpu.SemaphoreType.DMA((CHUNKS,)),
        ],
        compiler_params=pltpu.CompilerParams(vmem_limit_bytes=1024 * 1024),
        name="schedule",
    )(fdest, fsource, bdest, bsource, count, tiles)


def spread(table, tiles, sources, dests, start, outs, transposed):
    total, size = tiles.shape[:2]
    slots = dests + 1
    srcs = slots + room(total, dests)
    block = sources[0].shape
    n_in, n_out = len(sources), len(outs)
    groups_max = -(-n_in // GROUP)
    given = sum(outs)

    def body(*refs):
        table, tiles = refs[:2]
        ins = refs[2 : 2 + n_in]
        results = refs[2 + n_in : 2 + n_in + n_out]
        src, stage = refs[2 + n_in + n_out :]
        for k, ref in enumerate(ins):
            src[k] = ref[...]
        src[n_in] = jnp.zeros(block, BF)

        def product(p, n):
            held = [tiles[table[slots + p + k]] for k in range(n)]
            met = [src[table[srcs + p + k]] for k in range(n)]
            left, right = (met, held) if transposed else (held, met)
            return jnp.dot(
                jnp.concatenate(left, 1),
                jnp.concatenate(right, 0),
                preferred_element_type=F32,
            )

        def one(k, carry):
            lo = table[start + k]
            groups = table[start + k + 1] - lo
            for n in range(1, groups_max + 1):

                @pl.when(groups == n)
                def _():
                    stage[k] = product(lo * GROUP, n * GROUP).astype(BF)

            return carry

        lax.fori_loop(0, given, one, 0)
        at = 0
        for result, n in zip(results, outs):
            result[...] = stage[at : at + n] if n > 1 else stage[at]
            at += n

    flops = 2 * total * size * block[0] * block[1] * given // dests
    shapes = [((n,) if n > 1 else ()) + block for n in outs]
    return pl.pallas_call(
        body,
        in_specs=[SMEM] + [VMEM] * (1 + n_in),
        out_specs=[VMEM] * n_out,
        out_shape=[jax.ShapeDtypeStruct(s, BF) for s in shapes],
        scratch_shapes=[
            pltpu.VMEM((n_in + 1,) + block, BF),
            pltpu.VMEM((given,) + block, BF),
        ],
        compiler_params=pltpu.CompilerParams(vmem_limit_bytes=12 * 1024 * 1024),
        cost_estimate=pl.CostEstimate(
            flops=flops * 20, transcendentals=0, bytes_accessed=2 * total * size * size
        ),
        name="spread_back" if transposed else "spread",
    )(table, tiles, *sources)


def add_pairs(kept, met):
    n = kept.shape[0]

    def body(a, b, *outs):
        for k in range(n):
            outs[k][...] = a[k] + b[k]

    return pl.pallas_call(
        body,
        in_specs=[VMEM] * 2,
        out_specs=[VMEM] * n,
        out_shape=[jax.ShapeDtypeStruct(kept.shape[1:], BF)] * n,
        compiler_params=pltpu.CompilerParams(vmem_limit_bytes=1024 * 1024),
        name="add_pairs",
    )(kept, met)


def gather(block, axis, pair, step, between):
    far = lax.ppermute(block, axis, pair)
    near2 = lax.ppermute(block, axis, step(2))
    near1 = lax.ppermute(block, axis, step(3))
    near3 = lax.ppermute(block, axis, step(1))
    near2 = between(near2)
    far1 = lax.ppermute(far, axis, step(3))
    far3 = lax.ppermute(far, axis, step(1))
    far2 = lax.ppermute(near2, axis, pair)
    return [block, near1, near2, near3, far, far1, far2, far3]


def scatter(own, far, axis, pair, step):
    up = lax.ppermute(far[1], axis, step(1))
    down = lax.ppermute(far[3], axis, step(3))
    across = lax.ppermute(far[2], axis, pair)
    near1 = lax.ppermute(own[1], axis, step(1))
    near3 = lax.ppermute(own[3], axis, step(3))
    for_pair = far[0].astype(F32) + up.astype(F32) + down.astype(F32)
    for_two = own[2].astype(F32) + across.astype(F32)
    near2 = lax.ppermute(for_two.astype(BF), axis, step(2))
    met = lax.ppermute(for_pair.astype(BF), axis, pair)
    terms = [own[0], near1, near3, near2, met]
    return sum(t.astype(F32) for t in terms)


def local(adj_tiles, tile_rows, tile_cols, tile_counts, features, weight, node_grad):
    tiles = adj_tiles[0, 0]
    rows = tile_rows[0, 0]
    cols = tile_cols[0, 0]
    size = tiles.shape[1]
    row_devices = lax.axis_size("row")
    col_devices = lax.axis_size("col")
    half = col_devices // 2
    row_at = lax.axis_index("row")
    col_at = lax.axis_index("col")
    x_at, yh_at = row_at & 3, row_at >> 2
    core, z_at, yl_at = col_at & 1, (col_at >> 1) & 3, col_at >> 3
    places = (
        [core, 1 - core],
        [(z_at + k) & 3 for k in range(RING)],
        [yl_at, 1 - yl_at],
        ((RING - z_at) & 3) * (features.shape[1] // (2 * RING)),
        jnp.full((8, 128), core, jnp.int32),
        jnp.full((8, 128), yl_at, jnp.int32),
    )
    features, places = lax.optimization_barrier((features, places))
    tiles = pltpu.with_memory_space_constraint(tiles, pltpu.HBM)

    def along_x(k):
        return [(i, (i & 4) | ((i + k) & 3)) for i in range(row_devices)]

    def along_z(k):
        return [(i, (i & 9) | ((i + 2 * k) & 6)) for i in range(col_devices)]

    yh_swap = [(i, i ^ 4) for i in range(row_devices)]
    yl_swap = [(i, i ^ 8) for i in range(col_devices)]
    swap = [(i, i ^ 1) for i in range(col_devices)]

    r_ring, r_pair, r_core = ((rows >> 1) - z_at) & 3, (rows >> 3) ^ yl_at, (rows & 1) ^ core
    c_ring, c_pair = (cols - x_at) & 3, (cols >> 2) ^ yh_at
    lists = schedule(
        r_ring + 4 * (1 - r_core) + 8 * (1 - r_pair),
        c_ring + 4 * c_pair,
        c_ring + 4 * (1 - c_pair),
        r_ring + 4 * r_pair + 8 * r_core,
        tile_counts[0],
        tiles,
        col_devices,
        row_devices,
    )
    tied = []

    def meanwhile(near2):
        out, near2 = lax.optimization_barrier((lists, near2))
        tied.append(out)
        return near2

    column = gather(features, "row", yh_swap, along_x, meanwhile)
    forward, backward, held = tied.pop()
    pairs = []
    for start in (0, half):
        sent, kept = spread(forward, held, column, col_devices, start, (RING, RING), False)
        pairs.append(add_pairs(kept, lax.ppermute(sent, "col", swap)))
    agg = scatter(pairs[1], pairs[0], "col", yl_swap, along_z).astype(BF)

    pre = jnp.dot(agg, weight, preferred_element_type=F32)
    node_out = jax.nn.silu(pre).astype(BF)
    sigma = jax.nn.sigmoid(pre)
    dpre = (node_grad.astype(F32) * sigma * (1.0 + pre * (1.0 - sigma))).astype(BF)
    dagg = lax.dot_general(
        weight, dpre, (((1,), (1,)), ((), ())), preferred_element_type=F32
    ).astype(BF)
    scale = 1.0 / jnp.sqrt(jnp.float32(size * row_devices * col_devices))


    own = gather(dagg, "col", yl_swap, along_z, lambda near2: near2)
    other = [lax.ppermute(b, "col", swap) for b in own]
    term = lax.dot_general(agg, dpre, (((0,), (0,)), ((), ())), preferred_element_type=F32)
    backs = [
        spread(backward, held, own + other, row_devices, start, (1,) * RING, True)
        for start in (0, RING)
    ]
    feature_grad = scatter(backs[1], backs[0], "row", yh_swap, along_x).T.astype(BF)

    cores, rings, halves, turn, core_is, yl_is = places

    def split(block, n):
        return block.reshape((n, block.shape[0] // n) + block.shape[1:])

    def pick(cut, at):
        return lax.dynamic_index_in_dim(cut, at, 0, False, allow_negative_indices=False)

    cut = split(term * scale, 2)
    share = pick(cut, cores[0]) + lax.ppermute(pick(cut, cores[1]), "col", swap)
    cut = split(share, RING)
    share = pick(cut, rings[0]) + sum(
        lax.ppermute(pick(cut, rings[k]), "col", along_z(k)) for k in (2, 1, 3)
    )
    cut = split(share, 2)
    share = pick(cut, halves[0]) + lax.ppermute(pick(cut, halves[1]), "col", yl_swap)
    share = share + sum(lax.ppermute(share, "row", along_x(k)) for k in (2, 1, 3))
    share = share + lax.ppermute(share, "row", yh_swap)

    def doubled(block, bit, perm):
        met = lax.ppermute(block, "col", perm)
        return jnp.where(
            bit[0:1, 0:1] == 0,
            jnp.concatenate([block, met], 0),
            jnp.concatenate([met, block], 0),
        )

    share = doubled(share, yl_is, yl_swap)
    ring = [share] + [lax.ppermute(share, "col", along_z(RING - k)) for k in (1, 2, 3)]
    share = lax.dynamic_slice_in_dim(
        jnp.concatenate(ring + ring, 0), turn, RING * share.shape[0], allow_negative_indices=False
    )
    weight_grad = doubled(share, core_is, swap)
    return node_out, weight_grad, feature_grad


def solution(mesh):
    in_specs = (
        P("row", "col", None, None, None),
        P("row", "col", None),
        P("row", "col", None),
        P("row", "col"),
        P(("col", "row"), None),
        P(),
        P(("row", "col"), None),
    )
    out_specs = (P(("row", "col"), None), P(), P(("col", "row"), None))
    return jax.shard_map(local, mesh=mesh, in_specs=in_specs, out_specs=out_specs, check_vma=False)
```

```python
import jax
import jax.numpy as jnp
from jax import lax
from jax.experimental import pallas as pl
from jax.experimental.pallas import tpu as pltpu
from jax.sharding import PartitionSpec as P

BF = jnp.bfloat16
F32 = jnp.float32
GROUP = 2
RING = 4
CHUNKS = 8
SMEM = pl.BlockSpec(memory_space=pltpu.SMEM)
VMEM = pl.BlockSpec(memory_space=pltpu.VMEM)
HBM = pl.BlockSpec(memory_space=pltpu.HBM)


def room(total, dests):
    return total + dests * GROUP


def list_tiles(dest, source, count, total, dests, blank, table, fill):
    slots = dests + 1
    srcs = slots + room(total, dests)
    for d in range(dests):
        fill[d] = 0

    def tally(t, carry):
        fill[dest[t]] = fill[dest[t]] + 1
        return carry

    lax.fori_loop(0, count, tally, 0)

    def place(d, pos):
        table[d] = pos
        groups = jnp.maximum(lax.div(fill[d] + (GROUP - 1), GROUP), 1)
        fill[d] = pos * GROUP
        for k in range(GROUP):
            last = (pos + groups - 1) * GROUP + k
            table[slots + last] = 0
            table[srcs + last] = blank
        return pos + groups

    table[dests] = lax.fori_loop(0, dests, place, 0)

    def put(t, carry):
        d = dest[t]
        p = fill[d]
        fill[d] = p + 1
        table[slots + p] = t
        table[srcs + p] = source[t]
        return carry

    lax.fori_loop(0, count, put, 0)


def tile_copies(tiles, held, count, sem):
    total = tiles.shape[0]
    chunk = -(-total // CHUNKS)
    cuts = [(at, min(chunk, total - at)) for at in range(0, total, chunk)]
    copies = [
        pltpu.make_async_copy(tiles.at[pl.ds(at, n)], held.at[pl.ds(at, n)], sem.at[k])
        for k, (at, n) in enumerate(cuts)
    ]
    for (at, _), copy in zip(cuts, copies):
        pl.when(at < count)(copy.start)

    def wait():
        for (at, _), copy in zip(cuts, copies):
            pl.when(at < count)(copy.wait)

    return wait


def schedule(fdest, fsource, bdest, bsource, count, tiles, row_tiles, col_tiles):
    total = fdest.shape[0]

    def body(fd, fr, bd, br, n, tiles, forward, backward, held, fill, sem):
        wait = tile_copies(tiles, held, n[0], sem)
        list_tiles(fd, fr, n[0], total, row_tiles, col_tiles, forward, fill)
        list_tiles(bd, br, n[0], total, col_tiles, row_tiles, backward, fill)
        wait()

    def table(dests):
        return jax.ShapeDtypeStruct((dests + 1 + 2 * room(total, dests),), jnp.int32)

    return pl.pallas_call(
        body,
        in_specs=[SMEM] * 5 + [HBM],
        out_specs=[SMEM] * 2 + [VMEM],
        out_shape=[
            table(row_tiles),
            table(col_tiles),
            jax.ShapeDtypeStruct(tiles.shape, tiles.dtype),
        ],
        scratch_shapes=[
            pltpu.SMEM((max(row_tiles, col_tiles),), jnp.int32),
            pltpu.SemaphoreType.DMA((CHUNKS,)),
        ],
        compiler_params=pltpu.CompilerParams(vmem_limit_bytes=1024 * 1024),
        name="schedule",
    )(fdest, fsource, bdest, bsource, count, tiles)


def spread(table, tiles, sources, dests, start, outs, transposed):
    total, size = tiles.shape[:2]
    slots = dests + 1
    srcs = slots + room(total, dests)
    block = sources[0].shape
    n_in, n_out = len(sources), len(outs)
    groups_max = -(-n_in // GROUP)
    given = sum(outs)

    def body(*refs):
        table, tiles = refs[:2]
        ins = refs[2 : 2 + n_in]
        results = refs[2 + n_in : 2 + n_in + n_out]
        src, stage = refs[2 + n_in + n_out :]
        for k, ref in enumerate(ins):
            src[k] = ref[...]
        src[n_in] = jnp.zeros(block, BF)

        def product(p, n):
            held = [tiles[table[slots + p + k]] for k in range(n)]
            met = [src[table[srcs + p + k]] for k in range(n)]
            left, right = (met, held) if transposed else (held, met)
            return jnp.dot(
                jnp.concatenate(left, 1),
                jnp.concatenate(right, 0),
                preferred_element_type=F32,
            )

        def one(k, carry):
            lo = table[start + k]
            groups = table[start + k + 1] - lo
            for n in range(1, groups_max + 1):

                @pl.when(groups == n)
                def _():
                    stage[k] = product(lo * GROUP, n * GROUP).astype(BF)

            return carry

        lax.fori_loop(0, given, one, 0)
        at = 0
        for result, n in zip(results, outs):
            result[...] = stage[at : at + n] if n > 1 else stage[at]
            at += n

    flops = 2 * total * size * block[0] * block[1] * given // dests
    shapes = [((n,) if n > 1 else ()) + block for n in outs]
    return pl.pallas_call(
        body,
        in_specs=[SMEM] + [VMEM] * (1 + n_in),
        out_specs=[VMEM] * n_out,
        out_shape=[jax.ShapeDtypeStruct(s, BF) for s in shapes],
        scratch_shapes=[
            pltpu.VMEM((n_in + 1,) + block, BF),
            pltpu.VMEM((given,) + block, BF),
        ],
        compiler_params=pltpu.CompilerParams(vmem_limit_bytes=12 * 1024 * 1024),
        cost_estimate=pl.CostEstimate(
            flops=flops * 20, transcendentals=0, bytes_accessed=2 * total * size * size
        ),
        name="spread_back" if transposed else "spread",
    )(table, tiles, *sources)


def add_pairs(kept, met):
    n = kept.shape[0]

    def body(a, b, *outs):
        for k in range(n):
            outs[k][...] = a[k] + b[k]

    return pl.pallas_call(
        body,
        in_specs=[VMEM] * 2,
        out_specs=[VMEM] * n,
        out_shape=[jax.ShapeDtypeStruct(kept.shape[1:], BF)] * n,
        compiler_params=pltpu.CompilerParams(vmem_limit_bytes=1024 * 1024),
        name="add_pairs",
    )(kept, met)


def gather(block, axis, pair, step, between):
    far = lax.ppermute(block, axis, pair)
    near2 = lax.ppermute(block, axis, step(2))
    near1 = lax.ppermute(block, axis, step(3))
    near3 = lax.ppermute(block, axis, step(1))
    near2 = between(near2)
    far1 = lax.ppermute(far, axis, step(3))
    far3 = lax.ppermute(far, axis, step(1))
    far2 = lax.ppermute(near2, axis, pair)
    return [block, near1, near2, near3, far, far1, far2, far3]


def after(value, events):
    return lax.optimization_barrier((value, events))[0]


def scatter(own, far, axis, pair, step):
    up = lax.ppermute(far[1], axis, step(1))
    down = lax.ppermute(far[3], axis, step(3))
    across = lax.ppermute(far[2], axis, pair)
    near1 = lax.ppermute(own[1], axis, step(1))
    near3 = lax.ppermute(own[3], axis, step(3))
    for_pair = far[0].astype(F32) + up.astype(F32) + down.astype(F32)
    for_two = own[2].astype(F32) + across.astype(F32)
    near2 = lax.ppermute(for_two.astype(BF), axis, step(2))
    met = lax.ppermute(for_pair.astype(BF), axis, pair)
    terms = [own[0], near1, near3, near2, met]
    return sum(t.astype(F32) for t in terms), (up, down, across), (near1, near3)


def local(adj_tiles, tile_rows, tile_cols, tile_counts, features, weight, node_grad):
    tiles = adj_tiles[0, 0]
    rows = tile_rows[0, 0]
    cols = tile_cols[0, 0]
    size = tiles.shape[1]
    row_devices = lax.axis_size("row")
    col_devices = lax.axis_size("col")
    half = col_devices // 2
    row_at = lax.axis_index("row")
    col_at = lax.axis_index("col")
    x_at, yh_at = row_at & 3, row_at >> 2
    core, z_at, yl_at = col_at & 1, (col_at >> 1) & 3, col_at >> 3
    places = [
        [bit, 1 - bit, (1 - bit) * (features.shape[1] >> (k + 1))]
        for k, bit in enumerate((core, (z_at & 1) ^ (z_at >> 1), z_at >> 1))
    ]
    features, places = lax.optimization_barrier((features, places))
    tiles = pltpu.with_memory_space_constraint(tiles, pltpu.HBM)

    def along_x(k):
        return [(i, (i & 4) | ((i + k) & 3)) for i in range(row_devices)]

    def along_z(k):
        return [(i, (i & 9) | ((i + 2 * k) & 6)) for i in range(col_devices)]

    yh_swap = [(i, i ^ 4) for i in range(row_devices)]
    yl_swap = [(i, i ^ 8) for i in range(col_devices)]
    swap = [(i, i ^ 1) for i in range(col_devices)]

    r_ring, r_pair, r_core = ((rows >> 1) - z_at) & 3, (rows >> 3) ^ yl_at, (rows & 1) ^ core
    c_ring, c_pair = (cols - x_at) & 3, (cols >> 2) ^ yh_at
    lists = schedule(
        r_ring + 4 * (1 - r_core) + 8 * (1 - r_pair),
        c_ring + 4 * c_pair,
        c_ring + 4 * (1 - c_pair),
        r_ring + 4 * r_pair + 8 * r_core,
        tile_counts[0],
        tiles,
        col_devices,
        row_devices,
    )
    tied = []

    def meanwhile(near2):
        out, near2 = lax.optimization_barrier((lists, near2))
        tied.append(out)
        return near2

    column = gather(features, "row", yh_swap, along_x, meanwhile)
    forward, backward, held = tied.pop()
    pairs = []
    for start in (0, half):
        sent, kept = spread(forward, held, column, col_devices, start, (RING, RING), False)
        pairs.append(add_pairs(kept, lax.ppermute(sent, "col", swap)))
    agg, _, _ = scatter(pairs[1], pairs[0], "col", yl_swap, along_z)
    agg = agg.astype(BF)

    pre = jnp.dot(agg, weight, preferred_element_type=F32)
    node_out = jax.nn.silu(pre).astype(BF)
    sigma = jax.nn.sigmoid(pre)
    dpre = (node_grad.astype(F32) * sigma * (1.0 + pre * (1.0 - sigma))).astype(BF)
    dagg = lax.dot_general(
        weight, dpre, (((1,), (1,)), ((), ())), preferred_element_type=F32
    ).astype(BF)
    scale = 1.0 / jnp.sqrt(jnp.float32(size * row_devices * col_devices))


    own = gather(dagg, "col", yl_swap, along_z, lambda near2: near2)
    other = [lax.ppermute(b, "col", swap) for b in own]
    late_agg, late_dpre = after((agg, dpre), own[4])
    term = lax.dot_general(
        late_agg, late_dpre, (((0,), (0,)), ((), ())), preferred_element_type=F32
    )
    backs = [
        spread(backward, held, own + other, row_devices, start, (1,) * RING, True)
        for start in (0, RING)
    ]
    summed, for_far, for_own = scatter(backs[1], backs[0], "row", yh_swap, along_x)
    feature_grad = summed.T.astype(BF)

    def flips(axis, bits):
        n = row_devices if axis == "row" else col_devices
        return axis, [(i, i ^ bits) for i in range(n)]

    def halved(block, at, *way):
        cut = block.reshape((2, block.shape[0] // 2) + block.shape[1:])
        mine, yours = (
            lax.dynamic_index_in_dim(cut, k, 0, False, allow_negative_indices=False) for k in at
        )
        return mine + lax.ppermute(yours.astype(BF), *way).astype(F32)

    def doubled(block, at, *way):
        met = lax.ppermute(block, *way)
        rows = block.shape[0]
        both = jnp.concatenate([met, block, met], 0)
        return lax.dynamic_slice_in_dim(both, at[2], 2 * rows, allow_negative_indices=False)

    steps = list(zip(places, (1, 2, 6)))
    share = term * scale
    events = {2: own[5:], 4: backs[0], 6: (for_far, backs[1])}
    for k, (at, bits) in enumerate(steps):
        if k in events:
            share = after(share, events[k])
        share = halved(share, at[:2], *flips("col", bits))
    for k, way in enumerate((("col", 8), ("row", 4), ("row", 1), ("row", 3)), len(steps)):
        if k in events:
            share = after(share, events[k])
        share = share + lax.ppermute(share.astype(BF), *flips(*way)).astype(F32)
    share = share.astype(BF)
    for at, bits in reversed(steps):
        share = doubled(share, at, *flips("col", bits))
    weight_grad = share.astype(F32)
    return node_out, weight_grad, feature_grad


def solution(mesh):
    in_specs = (
        P("row", "col", None, None, None),
        P("row", "col", None),
        P("row", "col", None),
        P("row", "col"),
        P(("col", "row"), None),
        P(),
        P(("row", "col"), None),
    )
    out_specs = (P(("row", "col"), None), P(), P(("col", "row"), None))
    return jax.shard_map(local, mesh=mesh, in_specs=in_specs, out_specs=out_specs, check_vma=False)
```

```python
import jax
import jax.numpy as jnp
from jax import lax
from jax.experimental import pallas as pl
from jax.experimental.pallas import tpu as pltpu
from jax.sharding import PartitionSpec as P

BF = jnp.bfloat16
F32 = jnp.float32
GROUP = 2
RING = 4
CHUNKS = 8
SMEM = pl.BlockSpec(memory_space=pltpu.SMEM)
VMEM = pl.BlockSpec(memory_space=pltpu.VMEM)
HBM = pl.BlockSpec(memory_space=pltpu.HBM)


def room(total, dests):
    return total + dests * GROUP


def list_tiles(dest, source, count, total, dests, blank, table, fill):
    slots = dests + 1
    srcs = slots + room(total, dests)
    for d in range(dests):
        fill[d] = 0

    def tally(t, carry):
        fill[dest[t]] = fill[dest[t]] + 1
        return carry

    lax.fori_loop(0, count, tally, 0)

    def place(d, pos):
        table[d] = pos
        groups = jnp.maximum(lax.div(fill[d] + (GROUP - 1), GROUP), 1)
        fill[d] = pos * GROUP
        for k in range(GROUP):
            last = (pos + groups - 1) * GROUP + k
            table[slots + last] = 0
            table[srcs + last] = blank
        return pos + groups

    table[dests] = lax.fori_loop(0, dests, place, 0)

    def put(t, carry):
        d = dest[t]
        p = fill[d]
        fill[d] = p + 1
        table[slots + p] = t
        table[srcs + p] = source[t]
        return carry

    lax.fori_loop(0, count, put, 0)


def tile_copies(tiles, held, count, sem):
    total = tiles.shape[0]
    chunk = -(-total // CHUNKS)
    cuts = [(at, min(chunk, total - at)) for at in range(0, total, chunk)]
    copies = [
        pltpu.make_async_copy(tiles.at[pl.ds(at, n)], held.at[pl.ds(at, n)], sem.at[k])
        for k, (at, n) in enumerate(cuts)
    ]
    for (at, _), copy in zip(cuts, copies):
        pl.when(at < count)(copy.start)

    def wait():
        for (at, _), copy in zip(cuts, copies):
            pl.when(at < count)(copy.wait)

    return wait


def schedule(fdest, fsource, bdest, bsource, count, tiles, row_tiles, col_tiles):
    total = fdest.shape[0]

    def body(fd, fr, bd, br, n, tiles, forward, backward, held, fill, sem):
        wait = tile_copies(tiles, held, n[0], sem)
        list_tiles(fd, fr, n[0], total, row_tiles, col_tiles, forward, fill)
        list_tiles(bd, br, n[0], total, col_tiles, row_tiles, backward, fill)
        wait()

    def table(dests):
        return jax.ShapeDtypeStruct((dests + 1 + 2 * room(total, dests),), jnp.int32)

    return pl.pallas_call(
        body,
        in_specs=[SMEM] * 5 + [HBM],
        out_specs=[SMEM] * 2 + [VMEM],
        out_shape=[
            table(row_tiles),
            table(col_tiles),
            jax.ShapeDtypeStruct(tiles.shape, tiles.dtype),
        ],
        scratch_shapes=[
            pltpu.SMEM((max(row_tiles, col_tiles),), jnp.int32),
            pltpu.SemaphoreType.DMA((CHUNKS,)),
        ],
        compiler_params=pltpu.CompilerParams(vmem_limit_bytes=1024 * 1024),
        name="schedule",
    )(fdest, fsource, bdest, bsource, count, tiles)


def spread(table, tiles, sources, dests, start, outs, transposed):
    total, size = tiles.shape[:2]
    slots = dests + 1
    srcs = slots + room(total, dests)
    block = sources[0].shape
    n_in, n_out = len(sources), len(outs)
    groups_max = -(-n_in // GROUP)
    given = sum(outs)

    def body(*refs):
        table, tiles = refs[:2]
        ins = refs[2 : 2 + n_in]
        results = refs[2 + n_in : 2 + n_in + n_out]
        src, stage = refs[2 + n_in + n_out :]
        for k, ref in enumerate(ins):
            src[k] = ref[...]
        src[n_in] = jnp.zeros(block, BF)

        def product(p, n):
            held = [tiles[table[slots + p + k]] for k in range(n)]
            met = [src[table[srcs + p + k]] for k in range(n)]
            left, right = (met, held) if transposed else (held, met)
            return jnp.dot(
                jnp.concatenate(left, 1),
                jnp.concatenate(right, 0),
                preferred_element_type=F32,
            )

        def one(k, carry):
            lo = table[start + k]
            groups = table[start + k + 1] - lo
            for n in range(1, groups_max + 1):

                @pl.when(groups == n)
                def _():
                    stage[k] = product(lo * GROUP, n * GROUP).astype(BF)

            return carry

        lax.fori_loop(0, given, one, 0)
        at = 0
        for result, n in zip(results, outs):
            result[...] = stage[at : at + n] if n > 1 else stage[at]
            at += n

    flops = 2 * total * size * block[0] * block[1] * given // dests
    shapes = [((n,) if n > 1 else ()) + block for n in outs]
    return pl.pallas_call(
        body,
        in_specs=[SMEM] + [VMEM] * (1 + n_in),
        out_specs=[VMEM] * n_out,
        out_shape=[jax.ShapeDtypeStruct(s, BF) for s in shapes],
        scratch_shapes=[
            pltpu.VMEM((n_in + 1,) + block, BF),
            pltpu.VMEM((given,) + block, BF),
        ],
        compiler_params=pltpu.CompilerParams(vmem_limit_bytes=12 * 1024 * 1024),
        cost_estimate=pl.CostEstimate(
            flops=flops * 20, transcendentals=0, bytes_accessed=2 * total * size * size
        ),
        name="spread_back" if transposed else "spread",
    )(table, tiles, *sources)


def add_pairs(kept, met):
    n = kept.shape[0]

    def body(a, b, *outs):
        for k in range(n):
            outs[k][...] = a[k] + b[k]

    return pl.pallas_call(
        body,
        in_specs=[VMEM] * 2,
        out_specs=[VMEM] * n,
        out_shape=[jax.ShapeDtypeStruct(kept.shape[1:], BF)] * n,
        compiler_params=pltpu.CompilerParams(vmem_limit_bytes=1024 * 1024),
        name="add_pairs",
    )(kept, met)


def sum_turned(terms):
    rows, width = terms[0].shape

    def body(*refs):
        refs[-1][...] = sum(t[...].astype(F32) for t in refs[:-1]).T.astype(BF)

    return pl.pallas_call(
        body,
        in_specs=[VMEM] * len(terms),
        out_specs=VMEM,
        out_shape=jax.ShapeDtypeStruct((width, rows), BF),
        compiler_params=pltpu.CompilerParams(vmem_limit_bytes=4 * 1024 * 1024),
        name="sum_turned",
    )(*terms)


def gather(block, axis, pair, step, between):
    far = lax.ppermute(block, axis, pair)
    near2 = lax.ppermute(block, axis, step(2))
    near1 = lax.ppermute(block, axis, step(3))
    near3 = lax.ppermute(block, axis, step(1))
    near2 = between(near2)
    far1 = lax.ppermute(far, axis, step(3))
    far3 = lax.ppermute(far, axis, step(1))
    far2 = lax.ppermute(near2, axis, pair)
    return [block, near1, near2, near3, far, far1, far2, far3]


def after(value, events):
    return lax.optimization_barrier((value, events))[0]


def scatter(own, far, axis, pair, step):
    up = lax.ppermute(far[1], axis, step(1))
    down = lax.ppermute(far[3], axis, step(3))
    across = lax.ppermute(far[2], axis, pair)
    near1 = lax.ppermute(own[1], axis, step(1))
    near3 = lax.ppermute(own[3], axis, step(3))
    for_pair = far[0].astype(F32) + up.astype(F32) + down.astype(F32)
    for_two = own[2].astype(F32) + across.astype(F32)
    near2 = lax.ppermute(for_two.astype(BF), axis, step(2))
    met = lax.ppermute(for_pair.astype(BF), axis, pair)
    terms = [own[0], near1, near3, near2, met]
    return terms, (up, down, across), (near1, near3)


def local(adj_tiles, tile_rows, tile_cols, tile_counts, features, weight, node_grad):
    tiles = adj_tiles[0, 0]
    rows = tile_rows[0, 0]
    cols = tile_cols[0, 0]
    size = tiles.shape[1]
    row_devices = lax.axis_size("row")
    col_devices = lax.axis_size("col")
    half = col_devices // 2
    row_at = lax.axis_index("row")
    col_at = lax.axis_index("col")
    x_at, yh_at = row_at & 3, row_at >> 2
    core, z_at, yl_at = col_at & 1, (col_at >> 1) & 3, col_at >> 3
    places = [
        [bit, 1 - bit, (1 - bit) * (features.shape[1] >> (k + 1))]
        for k, bit in enumerate((core, (z_at & 1) ^ (z_at >> 1), z_at >> 1))
    ]
    features, places = lax.optimization_barrier((features, places))
    tiles = pltpu.with_memory_space_constraint(tiles, pltpu.HBM)

    def along_x(k):
        return [(i, (i & 4) | ((i + k) & 3)) for i in range(row_devices)]

    def along_z(k):
        return [(i, (i & 9) | ((i + 2 * k) & 6)) for i in range(col_devices)]

    yh_swap = [(i, i ^ 4) for i in range(row_devices)]
    yl_swap = [(i, i ^ 8) for i in range(col_devices)]
    swap = [(i, i ^ 1) for i in range(col_devices)]

    r_ring, r_pair, r_core = ((rows >> 1) - z_at) & 3, (rows >> 3) ^ yl_at, (rows & 1) ^ core
    c_ring, c_pair = (cols - x_at) & 3, (cols >> 2) ^ yh_at
    lists = schedule(
        r_ring + 4 * (1 - r_core) + 8 * (1 - r_pair),
        c_ring + 4 * c_pair,
        c_ring + 4 * (1 - c_pair),
        r_ring + 4 * r_pair + 8 * r_core,
        tile_counts[0],
        tiles,
        col_devices,
        row_devices,
    )
    tied = []

    def meanwhile(near2):
        out, near2 = lax.optimization_barrier((lists, near2))
        tied.append(out)
        return near2

    column = gather(features, "row", yh_swap, along_x, meanwhile)
    forward, backward, held = tied.pop()
    pairs = []
    for start in (0, half):
        sent, kept = spread(forward, held, column, col_devices, start, (RING, RING), False)
        pairs.append(add_pairs(kept, lax.ppermute(sent, "col", swap)))
    terms, _, _ = scatter(pairs[1], pairs[0], "col", yl_swap, along_z)
    agg = sum(t.astype(F32) for t in terms).astype(BF)

    pre = jnp.dot(agg, weight, preferred_element_type=F32)
    node_out = jax.nn.silu(pre).astype(BF)
    sigma = jax.nn.sigmoid(pre)
    dpre = (node_grad.astype(F32) * sigma * (1.0 + pre * (1.0 - sigma))).astype(BF)
    dagg = lax.dot_general(
        weight, dpre, (((1,), (1,)), ((), ())), preferred_element_type=F32
    ).astype(BF)
    scale = 1.0 / jnp.sqrt(jnp.float32(size * row_devices * col_devices))


    own = gather(dagg, "col", yl_swap, along_z, lambda near2: near2)
    other = [lax.ppermute(b, "col", swap) for b in own]
    late_agg, late_dpre = after((agg, dpre), own[4])
    term = lax.dot_general(
        late_agg, late_dpre, (((0,), (0,)), ((), ())), preferred_element_type=F32
    )
    backs = [
        spread(backward, held, own + other, row_devices, start, (1,) * RING, True)
        for start in (0, RING)
    ]
    terms, for_far, for_own = scatter(backs[1], backs[0], "row", yh_swap, along_x)
    feature_grad = sum_turned(terms)

    def flips(axis, bits):
        n = row_devices if axis == "row" else col_devices
        return axis, [(i, i ^ bits) for i in range(n)]

    def halved(block, at, *way):
        cut = block.reshape((2, block.shape[0] // 2) + block.shape[1:])
        mine, yours = (
            lax.dynamic_index_in_dim(cut, k, 0, False, allow_negative_indices=False) for k in at
        )
        return mine + lax.ppermute(yours.astype(BF), *way).astype(F32)

    def doubled(block, at, *way):
        met = lax.ppermute(block, *way)
        rows = block.shape[0]
        both = jnp.concatenate([met, block, met], 0)
        return lax.dynamic_slice_in_dim(both, at[2], 2 * rows, allow_negative_indices=False)

    steps = list(zip(places, (1, 2, 6)))
    share = term * scale
    events = {2: own[5:], 4: backs[0], 6: (for_far, backs[1])}
    for k, (at, bits) in enumerate(steps):
        if k in events:
            share = after(share, events[k])
        share = halved(share, at[:2], *flips("col", bits))
    for k, way in enumerate((("col", 8), ("row", 4), ("row", 1), ("row", 3)), len(steps)):
        if k in events:
            share = after(share, events[k])
        share = share + lax.ppermute(share.astype(BF), *flips(*way)).astype(F32)
    share = share.astype(BF)
    for at, bits in reversed(steps):
        share = doubled(share, at, *flips("col", bits))
    weight_grad = share.astype(F32)
    return node_out, weight_grad, feature_grad


def solution(mesh):
    in_specs = (
        P("row", "col", None, None, None),
        P("row", "col", None),
        P("row", "col", None),
        P("row", "col"),
        P(("col", "row"), None),
        P(),
        P(("row", "col"), None),
    )
    out_specs = (P(("row", "col"), None), P(), P(("col", "row"), None))
    return jax.shard_map(local, mesh=mesh, in_specs=in_specs, out_specs=out_specs, check_vma=False)
```
